32 devices in a mesh: replica: 8 (over y, x, core), shard: 4 (over z).
Axes of the slice: x: 2, y: 2, z: 4, core: 2. Of those that a mesh axis runs over, the one named last changes fastest.
Arguments:
- inputs: float32 [64, 512, 1024], P(('replica', 'shard')), may hold values from -6 to 6
- lengths: int32 [64], P(('replica', 'shard')), may hold values from 1 to 512, 24576 in all
- cotangent: float32 [64, 512, 1024], P(('replica', 'shard')), may hold values from -6 to 6
- w_in: bfloat16 [2, 1024, 4384], P(None, 'shard'), may hold values from -0.1875 to 0.1875
- w_out: bfloat16 [2, 2048, 1024], P(None, 'shard'), may hold values from -0.125 to 0.125
- norm_gain: float32 [2, 1024], replicated, may hold values from 0.5 to 1.5
- conv_weight: float32 [2, 4, 2304], replicated, may hold values from -3 to 3
- conv_bias: float32 [2, 2304], replicated, may hold values from -3 to 3
- gate_gain: float32 [2, 2048], replicated, may hold values from 0.5 to 1.5
- dt_bias: float32 [2, 32], replicated, may hold values from -6.9 to -2.3
- a_log: float32 [2, 32], replicated, may hold values from 0 to 2.77
- skip: float32 [2, 32], replicated, may hold values from 0.5 to 1.5
Outputs:
- output: float32 [64, 512, 1024], P(('replica', 'shard'))
- input_grad: float32 [64, 512, 1024], P(('replica', 'shard'))
- grad_w_in: float32 [2, 1024, 4384], P(None, 'shard')
- grad_w_out: float32 [2, 2048, 1024], P(None, 'shard')
- grad_norm_gain: float32 [2, 1024], replicated
- grad_conv_weight: float32 [2, 4, 2304], replicated
- grad_conv_bias: float32 [2, 2304], replicated
- grad_gate_gain: float32 [2, 2048], replicated
- grad_dt_bias: float32 [2, 32], replicated
- grad_a_log: float32 [2, 32], replicated
- grad_skip: float32 [2, 32], replicated
The draws below stay inside these ranges and needn't reach their ends.
Inputs may be any that keep to these rules, and one draw needn't show every extreme that they name: `lengths`: every sequence has at least one token; the longest in each draw has exactly 512.
All inputs are finite; a program needn't handle non-finite values. No bound on the sum of `lengths` on one device may be relied on, other than what follows from the above.
Results may differ from the reference program's by a relative error of at most 0.028.
Values may be sent and summed in bfloat16 or wider, within the bound.
No kernel may reach another device: no remote copies, remote signals or barrier semaphores. Data moves between devices by JAX's collectives and lax.ppermute only.
A program may use at most 320 MiB of HBM per device.

```python
import math
import jax
import jax.numpy as jnp
import numpy as np
from jax import lax

D = 1024
DI = 2048
HEADS = 32
HEAD_DIM = 64
STATE = 128
CONV = 4
SPAN = 256
LEN = 512
LAYERS = 2
EIN = 4384
SEQS = 64


def steps_of(rng, dims, pieces, low, largest):
    level = 1.0
    for dim, blocks in pieces:
        heights = jax.random.uniform(jax.random.fold_in(jax.random.fold_in(rng, 6), dim), (blocks,), jnp.float32, low / len(pieces), largest / len(pieces))
        level = level * jnp.repeat(jnp.exp(heights), dims[dim] // blocks).reshape((-1,) + (1,) * (len(dims) - 1 - dim))
    return level


def split_up(count, total, limit, skew):
    loads = [(1 << 20) // math.isqrt(rank ** skew) + 1 for rank in range(2, count + 1)]
    rest, holding = total - limit - (count - 1), [1] * (count - 1)
    while rest > 0:
        movable = [i for i in range(count - 1) if holding[i] < limit]
        whole, left = sum([loads[i] for i in movable]), rest
        for i in movable:
            extra = min(limit - holding[i], max(1, left * loads[i] // whole), rest)
            holding[i] = holding[i] + extra
            rest = rest - extra
    return np.array([limit] + holding)


def ragged(stream_key, number_of, total, bound, skew):
    if number_of == 2:
        one = jax.random.randint(stream_key, (), max(1, total - bound), min(bound, total - 1) + 1)
        return jnp.stack([one, total - one])
    tallies = jnp.asarray(split_up(number_of, total, bound, skew), jnp.int32)
    couples = (number_of - 1) // 2
    source_of, receiver = tallies[1:1 + 2 * couples:2], tallies[2:2 + 2 * couples:2]
    margin = jnp.minimum(source_of - 1, bound - receiver)
    passed = jax.random.randint(jax.random.fold_in(stream_key, 1), (couples,), 0, 1 << 20) % (margin + 1)
    tallies = tallies.at[1:1 + 2 * couples:2].set(source_of - passed).at[2:2 + 2 * couples:2].set(receiver + passed)
    return tallies[jax.random.permutation(jax.random.fold_in(stream_key, 2), number_of)]


def bell_draw(stream_key, shape, spread, reach, cuts=(), dtype=jnp.bfloat16):
    drawn = jax.random.normal(stream_key, shape, jnp.float32) * spread
    if len(cuts) > 0:
        drawn = steps_of(stream_key, shape, cuts, -0.22, 0.18) * drawn
    return jnp.clip(drawn, min=-reach, max=reach).astype(dtype)


def setup_inputs(seed: int = 0) -> dict:
    streams_of = jax.random.split(jax.random.key(seed), 13)
    return {
        "inputs": bell_draw(streams_of[0], (SEQS, LEN, D), 1.0, 6.0, ((0, 32),), jnp.float32),
        "lengths": ragged(streams_of[1], SEQS, SEQS * LEN * 3 // 4, LEN, 2).astype(jnp.int32),
        "cotangent": bell_draw(streams_of[2], (SEQS, LEN, D), 1.0, 6.0, ((0, 32),), jnp.float32),
        "w_in": bell_draw(streams_of[3], (LAYERS, D, EIN), D ** -0.5, 0.1875, ((1, 4),)),
        "w_out": bell_draw(streams_of[4], (LAYERS, DI, D), DI ** -0.5, 0.125, ((1, 4),)),
        "norm_gain": jnp.clip(1.0 + 0.1 * jax.random.normal(streams_of[5], (LAYERS, D), jnp.float32), 0.5, 1.5),
        "conv_weight": bell_draw(streams_of[6], (LAYERS, CONV, DI + 2 * STATE), CONV ** -0.5, 3.0, (), jnp.float32),
        "conv_bias": bell_draw(streams_of[7], (LAYERS, DI + 2 * STATE), 0.5, 3.0, (), jnp.float32),
        "gate_gain": jnp.clip(1.0 + 0.1 * jax.random.normal(streams_of[8], (LAYERS, DI), jnp.float32), 0.5, 1.5),
        "dt_bias": jnp.clip(jax.random.uniform(streams_of[9], (LAYERS, HEADS), jnp.float32, -6.9, -2.3), -6.9, -2.3),
        "a_log": jnp.clip(jax.random.uniform(streams_of[10], (LAYERS, HEADS), jnp.float32, 0.0, 2.77), 0.0, 2.77),
        "skip": jnp.clip(jax.random.uniform(streams_of[11], (LAYERS, HEADS), jnp.float32, 0.5, 1.5), 0.5, 1.5),
    }


EPSILON = 1e-05
HIGHEST = lax.Precision.HIGHEST

@jax.custom_vjp
def low(v):
    return lax.optimization_barrier(v.astype(jnp.bfloat16)).astype(jnp.float32)

@jax.custom_vjp
def low_back(v):
    return v

def low_keep(v):
    return (low(v), None)

def low_pass(kept, grad):
    return (grad,)

def back_keep(v):
    return (v, None)

def back_low(kept, grad):
    return (low(grad),)
low.defvjp(low_keep, low_pass)
low_back.defvjp(back_keep, back_low)

def rms_scale(values, gain):
    return values * lax.rsqrt(lax.optimization_barrier(jnp.mean(values * values, axis=-1, keepdims=True)) + EPSILON) * gain

def span_scan(inner_x, step_size, rate, b_input, c_output):
    seq_len = inner_x.shape[0]
    blocks = seq_len // SPAN
    logs = (step_size * rate[None, :]).reshape(blocks, SPAN, HEADS)
    cum_logs = jnp.cumsum(logs, axis=1)
    scaled_x = (inner_x * step_size[:, :, None]).reshape(blocks, SPAN, HEADS, HEAD_DIM)
    b_blocks = b_input.reshape(blocks, SPAN, STATE)
    c_blocks = c_output.reshape(blocks, SPAN, STATE)
    scores = jnp.einsum('cqn,ckn->cqk', c_blocks, b_blocks, precision=HIGHEST)
    row_index = lax.broadcasted_iota(jnp.int32, (SPAN, SPAN), 0)
    col_index = lax.broadcasted_iota(jnp.int32, (SPAN, SPAN), 1)
    causal = (row_index >= col_index)[None, None, :, :]
    cum_heads = jnp.transpose(cum_logs, (0, 2, 1))
    log_gaps = cum_heads[:, :, :, None] - cum_heads[:, :, None, :]
    decays = jnp.where(causal, jnp.exp(jnp.where(causal, log_gaps, 0.0)), 0.0)
    mixing = decays * scores[:, None, :, :]
    intra = jnp.einsum('chqk,ckhp->cqhp', mixing, scaled_x, precision=HIGHEST)
    to_end = jnp.exp(cum_logs[:, -1:, :] - cum_logs)
    states = jnp.einsum('ckhp,ckn->chpn', scaled_x * to_end[:, :, :, None], b_blocks, precision=HIGHEST)
    totals = jnp.exp(cum_logs[:, -1, :])
    carried = jnp.zeros((HEADS, HEAD_DIM, STATE), jnp.float32)
    previous = []
    for block in range(blocks):
        previous.append(carried)
        carried = totals[block][:, None, None] * carried + states[block]
    previous = jnp.stack(previous)
    inter = jnp.einsum('cqn,chpn->cqhp', c_blocks, previous, precision=HIGHEST) * jnp.exp(cum_logs)[:, :, :, None]
    return (intra + inter).reshape(seq_len, HEADS, HEAD_DIM)

def mix_one(projected, conv_weight, conv_bias, gate_gain, dt_bias, a_log, skip):
    seq_len = projected.shape[0]
    gate_part = projected[:, :DI]
    conv_in = projected[:, DI:2 * DI + 2 * STATE]
    raw_step = projected[:, 2 * DI + 2 * STATE:]
    padded = jnp.pad(conv_in, ((CONV - 1, 0), (0, 0)))
    pre_act = conv_bias[None, :] + conv_weight[0][None, :] * padded[0:seq_len]
    for offset in range(1, CONV):
        pre_act = pre_act + conv_weight[offset][None, :] * padded[offset:offset + seq_len]
    act = jax.nn.silu(pre_act)
    inner_x = act[:, :DI].reshape(seq_len, HEADS, HEAD_DIM)
    b_input = act[:, DI:DI + STATE]
    c_output = act[:, DI + STATE:]
    step_size = jax.nn.softplus(raw_step + dt_bias[None, :])
    scanned = span_scan(inner_x, step_size, -jnp.exp(a_log), b_input, c_output)
    scanned = scanned + skip[None, :, None] * inner_x
    gated = scanned.reshape(seq_len, DI) * jax.nn.silu(gate_part)
    return rms_scale(gated, gate_gain)

def layer_apply(hidden, valid_mask, w_in, w_out, norm_gain, conv_weight, conv_bias, gate_gain, dt_bias, a_log, skip):
    normed = low(rms_scale(hidden, norm_gain))
    projected = low_back(jnp.einsum('bld,de->ble', normed, w_in, precision=HIGHEST))
    one_seq = jax.checkpoint(lambda row: mix_one(row, conv_weight, conv_bias, gate_gain, dt_bias, a_log, skip))
    mixed = low(lax.map(one_seq, projected))
    branch = low_back(jnp.einsum('bli,id->bld', mixed, w_out, precision=HIGHEST))
    return hidden + valid_mask[:, :, None] * branch

def forward(hidden, valid_mask, params):
    for layer in range(LAYERS):
        hidden = layer_apply(hidden, valid_mask, *[item[layer] for item in params])
    return hidden

def reference(inputs, lengths, cotangent, w_in, w_out, norm_gain, conv_weight, conv_bias, gate_gain, dt_bias, a_log, skip):
    params = (w_in.astype(jnp.float32), w_out.astype(jnp.float32), norm_gain, conv_weight, conv_bias, gate_gain, dt_bias, a_log, skip)
    group_size = 4
    groups = SEQS // group_size
    places = lax.broadcasted_iota(jnp.int32, (SEQS, LEN), 1)
    valid_mask = (places < lengths[:, None]).astype(jnp.float32)
    grouped = (inputs.reshape(groups, group_size, LEN, D), valid_mask.reshape(groups, group_size, LEN), cotangent.reshape(groups, group_size, LEN, D))

    def scan_step(totals, item):
        group_in, group_mask, group_cot = item
        result, pull = jax.vjp(lambda values, weights: forward(values, group_mask, weights), group_in, params)
        d_input, d_params = pull(group_cot)
        totals = jax.tree.map(lambda left, right: left + right, totals, d_params)
        return (totals, (result, d_input))
    zeros = jax.tree.map(lambda item: jnp.zeros(item.shape, jnp.float32), params)
    totals, (results, d_inputs) = lax.scan(scan_step, zeros, grouped)
    return (results.reshape(SEQS, LEN, D), d_inputs.reshape(SEQS, LEN, D), totals[0], totals[1], totals[2], totals[3], totals[4], totals[5], totals[6], totals[7], totals[8])
```

```python
import jax
import jax.numpy as jnp
from jax import lax
from jax.experimental import pallas as pl
from jax.experimental.pallas import tpu as pltpu
from jax.sharding import Mesh
from jax.sharding import PartitionSpec as P

DI = 2048
HEADS = 32
HEAD_DIM = 64
STATE = 128
CONV = 4
EPSILON = 1e-05
CHUNK = 128
PAIR = 2 * HEAD_DIM
LOG2E = 1.4426950408889634
BF = jnp.bfloat16
F32 = jnp.float32


def dot_f32(left, right, dims, precision=None):
    return lax.dot_general(
        left, right, (dims, ((), ())), preferred_element_type=F32, precision=precision
    )


def mm(left, right):
    return dot_f32(left, right, ((1,), (0,)))


def mm_nt(left, right):
    return dot_f32(left, right, ((1,), (1,)))


def mm_tn(left, right):
    return dot_f32(left, right, ((0,), (0,)))


def split_two(values):
    high = values.astype(BF)
    low = (values - high.astype(F32)).astype(BF)
    return high, low


def block_diag(pair):
    lane = lax.broadcasted_iota(jnp.int32, pair.shape, 1)
    zero = jnp.zeros_like(pair)
    return jnp.concatenate(
        [jnp.where(lane < HEAD_DIM, pair, zero), jnp.where(lane >= HEAD_DIM, pair, zero)], axis=0
    )


def sigmoid(values):
    return 1.0 / (1.0 + jnp.exp(-values))


def softplus(values):
    return jnp.maximum(values, 0.0) + jnp.log1p(jnp.exp(-jnp.abs(values)))


def conv_pre(ext_ref, cw_ref, cb_ref, cols):
    total = cb_ref[:, cols] + cw_ref[0:1, cols] * ext_ref[5 : 5 + CHUNK, cols]
    for tap in range(1, CONV):
        total = total + cw_ref[tap : tap + 1, cols] * ext_ref[5 + tap : 5 + tap + CHUNK, cols]
    return total


def head_terms(raw_ref, dtb_ref, al_ref, spread_ref):
    shifted = raw_ref[...] + dtb_ref[...]
    step = softplus(shifted)
    rate = -jnp.exp(al_ref[...])
    row = lax.broadcasted_iota(jnp.int32, (CHUNK, CHUNK), 0)
    col = lax.broadcasted_iota(jnp.int32, (CHUNK, CHUNK), 1)
    lower = (row >= col).astype(F32)
    cum = dot_f32(lower, step * (rate * LOG2E), ((1,), (0,)), lax.Precision.HIGHEST)
    to_end = jnp.exp2(cum[CHUNK - 1 : CHUNK, :] - cum)

    def spread(values):
        high, low = split_two(values)
        return mm(jnp.concatenate([high, low], axis=1), spread_ref[...])

    return shifted, step, rate, cum, spread(step), spread(to_end), spread(jnp.exp2(cum))


def fwd_body(
    proj_ref, raw_ref, cw_ref, cb_ref, gg_ref, dtb_ref, al_ref, sk_ref, spread_ref,
    mixed_ref, y_ref, entry_ref,
    state, ext, gated,
):
    chunk = pl.program_id(1)

    @pl.when(chunk == 0)
    def _():
        state[...] = jnp.zeros_like(state)
        ext[0:8, :] = jnp.zeros((8, ext.shape[1]), F32)

    @pl.when(chunk != 0)
    def _():
        ext[0:8, :] = ext[CHUNK : CHUNK + 8, :]

    ext[8 : 8 + CHUNK, :] = proj_ref[:, DI : 2 * DI + 2 * STATE].astype(F32)

    def act(start, width):
        pre = conv_pre(ext, cw_ref, cb_ref, slice(start, start + width))
        return pre * sigmoid(pre)

    b_low = act(DI, STATE).astype(BF)
    c_low = act(DI + STATE, STATE).astype(BF)
    _, _, _, cum, step_x, end_x, ecum_x = head_terms(raw_ref, dtb_ref, al_ref, spread_ref)
    cum_t = cum.T
    row = lax.broadcasted_iota(jnp.int32, (CHUNK, CHUNK), 0)
    col = lax.broadcasted_iota(jnp.int32, (CHUNK, CHUNK), 1)
    scores = jnp.where(row >= col, mm_nt(c_low, b_low), 0.0)
    entry_low = state[...].astype(BF)
    entry_ref[0] = entry_low
    b_t = b_low.astype(F32).T.astype(BF)
    squares = jnp.zeros((CHUNK, PAIR), F32)
    for pair in range(HEADS // 2):
        cols = slice(pair * PAIR, (pair + 1) * PAIR)
        x = act(pair * PAIR, PAIR)
        x_step = x * step_x[:, cols]
        mixing = []
        for head in (2 * pair, 2 * pair + 1):
            gap = jnp.minimum(cum[:, head : head + 1] - cum_t[head : head + 1, :], 0.0)
            mixing.append((jnp.exp2(gap) * scores).astype(BF))
        intra = mm(jnp.concatenate(mixing, axis=1), block_diag(x_step.astype(BF)))
        inter = mm(c_low, entry_low[:, cols]) * ecum_x[:, cols]
        y = intra + inter + sk_ref[:, cols] * x
        y_ref[:, cols] = y.astype(BF)
        grown = mm(b_t, (x_step * end_x[:, cols]).astype(BF))
        state[:, cols] = state[:, cols] * ecum_x[CHUNK - 1 : CHUNK, cols] + grown
        z = proj_ref[:, cols].astype(F32)
        g = y * (z * sigmoid(z))
        gated[:, cols] = g
        squares = squares + g * g
    scale = lax.rsqrt(jnp.sum(squares, axis=1, keepdims=True) * (1.0 / DI) + EPSILON)
    for pair in range(HEADS // 2):
        cols = slice(pair * PAIR, (pair + 1) * PAIR)
        mixed_ref[:, cols] = (gated[:, cols] * scale * gg_ref[:, cols]).astype(BF)


def bwd_body(
    proj_ref, before_ref, raw_ref, y_ref, entry_ref, dmix_ref,
    cw_ref, cb_ref, gg_ref, dtb_ref, al_ref, sk_ref, spread_ref, gather_ref,
    cw0_ref, cb0_ref, gg0_ref, sk0_ref, dtb0_ref, al0_ref,
    dproj_ref, dcw_ref, dcb_ref, dgg_ref, dsk_ref, ddtb_ref, dal_ref,
    adj, ext, dpre, act_s, slope_s, dy_s, da_high, da_low, u_s,
):
    turn = pl.program_id(0)
    last = pl.num_programs(0) - 1

    @pl.when(turn == 0)
    def _():
        dcw_ref[...] = cw0_ref[...]
        dcb_ref[...] = cb0_ref[...]
        dgg_ref[...] = gg0_ref[...]
        dsk_ref[...] = sk0_ref[...]
        ddtb_ref[...] = dtb0_ref[...]
        dal_ref[...] = al0_ref[...]

    @pl.when(turn == 0)
    def _():
        adj[...] = jnp.zeros_like(adj)
        dpre[CHUNK : CHUNK + 8, :] = jnp.zeros((8, dpre.shape[1]), F32)

    ext[0:8, :] = jnp.where(
        turn == last, 0.0, before_ref[8:16, DI : 2 * DI + 2 * STATE].astype(F32)
    )
    ext[8 : 8 + CHUNK, :] = proj_ref[:, DI : 2 * DI + 2 * STATE].astype(F32)
    conv_width = DI + 2 * STATE
    for start in range(0, conv_width, PAIR):
        cols = slice(start, start + PAIR)
        pre = conv_pre(ext, cw_ref, cb_ref, cols)
        sig = sigmoid(pre)
        act = pre * sig
        act_s[:, cols] = act
        slope_s[:, cols] = sig + act * (1.0 - sig)

    squares = jnp.zeros((CHUNK, PAIR), F32)
    crossed = jnp.zeros((CHUNK, PAIR), F32)
    for pair in range(HEADS // 2):
        cols = slice(pair * PAIR, (pair + 1) * PAIR)
        z = proj_ref[:, cols].astype(F32)
        g = y_ref[:, cols].astype(F32) * (z * sigmoid(z))
        squares = squares + g * g
        crossed = crossed + dmix_ref[:, cols].astype(F32) * gg_ref[:, cols] * g
    scale = lax.rsqrt(jnp.sum(squares, axis=1, keepdims=True) * (1.0 / DI) + EPSILON)
    pull = scale * scale * scale * (jnp.sum(crossed, axis=1, keepdims=True) * (1.0 / DI))
    for pair in range(HEADS // 2):
        cols = slice(pair * PAIR, (pair + 1) * PAIR)
        z = proj_ref[:, cols].astype(F32)
        y = y_ref[:, cols].astype(F32)
        d_mixed = dmix_ref[:, cols].astype(F32)
        sig = sigmoid(z)
        silu = z * sig
        g = y * silu
        scaled = d_mixed * scale
        d_gated = scaled * gg_ref[:, cols] - g * pull
        dgg_ref[:, cols] += jnp.sum(scaled * g, axis=0, keepdims=True)
        dy_s[:, cols] = d_gated * silu
        dproj_ref[:, cols] = (d_gated * y * (sig + silu * (1.0 - sig))).astype(BF)

    b_low = act_s[:, DI : DI + STATE].astype(BF)
    c_low = act_s[:, DI + STATE :].astype(BF)
    shifted, step, rate, cum, step_x, end_x, ecum_x = head_terms(
        raw_ref, dtb_ref, al_ref, spread_ref
    )
    cum_t = cum.T
    row = lax.broadcasted_iota(jnp.int32, (CHUNK, CHUNK), 0)
    col = lax.broadcasted_iota(jnp.int32, (CHUNK, CHUNK), 1)
    raw_scores = mm_nt(c_low, b_low)
    scores = jnp.where(row >= col, raw_scores, 0.0)
    scores_t = scores.T
    c_t = c_low.astype(F32).T.astype(BF)
    d_scores = jnp.zeros((CHUNK, CHUNK), F32)
    d_c = jnp.zeros((CHUNK, STATE), F32)
    d_b = jnp.zeros((CHUNK, STATE), F32)
    crossing = []
    for pair in range(HEADS // 2):
        cols = slice(pair * PAIR, (pair + 1) * PAIR)
        x = act_s[:, cols]
        dy = dy_s[:, cols]
        step_p = step_x[:, cols]
        x_step = x * step_p
        x_low = x_step.astype(BF)
        dy_low = dy.astype(BF)
        x_bd = block_diag(x_low)
        g_both = mm_nt(dy_low, x_bd)
        mixing = []
        mixing_t = []
        for place, head in enumerate((2 * pair, 2 * pair + 1)):
            down = cum[:, head : head + 1]
            across = cum_t[head : head + 1, :]
            decay = jnp.exp2(jnp.minimum(down - across, 0.0))
            mixing.append((decay * scores).astype(BF))
            d_scores = d_scores + decay * g_both[:, place * CHUNK : (place + 1) * CHUNK]
            decay_t = jnp.exp2(jnp.minimum(across - down, 0.0))
            mixing_t.append((decay_t * scores_t).astype(BF))
        intra = mm(jnp.concatenate(mixing, axis=1), x_bd)
        spread_dy = mm(jnp.concatenate(mixing_t, axis=1), block_diag(dy_low))
        entry = entry_ref[0, :, cols]
        adj_p = adj[:, cols]
        adj_low = adj_p.astype(BF)
        ecum_p = ecum_x[:, cols]
        end_p = end_x[:, cols]
        from_end = mm(b_low, adj_low) * end_p
        y_scan = intra + mm(c_low, entry) * ecum_p
        stuff = spread_dy + from_end
        x_round = x_low.astype(F32)
        u = x_round * stuff
        high, low = split_two(dy_low.astype(F32) * y_scan - u)
        da_high[:, cols] = high
        da_low[:, cols] = low
        u_s[:, cols] = u.astype(BF)
        dy_e = (dy * ecum_p).astype(BF)
        x_e = (x_step * end_p).astype(BF)
        d_c = d_c + mm_nt(dy_e, entry)
        d_b = d_b + mm_nt(x_e, adj_low)
        ecum_last = ecum_x[CHUNK - 1 : CHUNK, cols]
        crossing.append(
            jnp.sum(x_round * from_end, axis=0, keepdims=True)
            + ecum_last * jnp.sum(adj_p * entry.astype(F32), axis=0, keepdims=True)
        )
        adj[:, cols] = adj_p * ecum_last + mm(c_t, dy_e)
        dsk_ref[:, cols] += jnp.sum(dy * x, axis=0, keepdims=True)
        dpre[0:CHUNK, cols] = (step_p * stuff + sk_ref[:, cols] * dy) * slope_s[:, cols]

    through = mm(da_high[...], gather_ref[...]) + mm(da_low[...], gather_ref[...])
    u_head = mm(u_s[...], gather_ref[...])[:, :HEADS]
    cross_row = jnp.broadcast_to(jnp.concatenate(crossing, axis=1), (16, DI))
    cross_high, cross_low = split_two(cross_row)
    cross = (mm(cross_high, gather_ref[...]) + mm(cross_low, gather_ref[...]))[0:1, :HEADS]
    upper = (row <= col).astype(F32)
    d_log = dot_f32(upper, through[:, :HEADS], ((1,), (0,)), lax.Precision.HIGHEST) + cross
    sig = sigmoid(shifted)
    ratio = jnp.where(step > 1e-30, sig / step, 1.0)
    d_raw = u_head * ratio + rate * d_log * sig
    dproj_ref[:, 2 * DI + 2 * STATE :] = d_raw.astype(BF)
    ddtb_ref[...] += jnp.sum(d_raw, axis=0, keepdims=True)
    dal_ref[...] += rate * jnp.sum(step * d_log, axis=0, keepdims=True)

    d_scores = jnp.where(row >= col, d_scores, 0.0)
    d_c = d_c + mm(d_scores.astype(BF), b_low)
    d_b = d_b + mm(d_scores.T.astype(BF), c_low)
    dpre[0:CHUNK, DI : DI + STATE] = d_b * slope_s[:, DI : DI + STATE]
    dpre[0:CHUNK, DI + STATE :] = d_c * slope_s[:, DI + STATE :]
    for start in range(0, conv_width, PAIR):
        cols = slice(start, start + PAIR)
        here = dpre[0:CHUNK, cols]
        d_conv = cw_ref[CONV - 1 : CONV, cols] * here
        dcb_ref[:, cols] += jnp.sum(here, axis=0, keepdims=True)
        for tap in range(CONV):
            dcw_ref[tap : tap + 1, cols] += jnp.sum(
                here * ext[5 + tap : 5 + tap + CHUNK, cols], axis=0, keepdims=True
            )
            if tap < CONV - 1:
                ahead = CONV - 1 - tap
                d_conv = d_conv + cw_ref[tap : tap + 1, cols] * dpre[ahead : ahead + CHUNK, cols]
        dproj_ref[:, DI + start : DI + start + PAIR] = d_conv.astype(BF)
    dpre[CHUNK : CHUNK + 8, :] = dpre[0:8, :]


def head_maps():
    head = jnp.arange(DI) // HEAD_DIM
    spread = (jnp.arange(HEADS)[:, None] == head[None, :]).astype(BF)
    gather = (head[:, None] == jnp.arange(128)[None, :]).astype(BF)
    return jnp.concatenate([spread, spread], axis=0), gather


def whole(array):
    return pl.BlockSpec(array.shape, lambda seq, turn: (0,) * array.ndim)


def param_rows(extras):
    conv_weight, conv_bias, gate_gain, dt_bias, a_log, skip = extras
    return (
        conv_weight,
        conv_bias[None, :],
        gate_gain[None, :],
        dt_bias[None, :],
        a_log[None, :],
        jnp.repeat(skip, HEAD_DIM)[None, :],
    )


def mix_forward(proj, raw, extras, seq_len):
    rows = proj.shape[0]
    seqs, chunks = rows // seq_len, seq_len // CHUNK
    params = param_rows(extras) + (head_maps()[0],)

    def at(width):
        return pl.BlockSpec((CHUNK, width), lambda seq, turn: (seq * chunks + turn, 0))

    conv_width = DI + 2 * STATE
    return pl.pallas_call(
        fwd_body,
        grid=(seqs, chunks),
        in_specs=[at(proj.shape[1]), at(HEADS)] + [whole(item) for item in params],
        out_specs=[
            at(DI),
            at(DI),
            pl.BlockSpec((1, STATE, DI), lambda seq, turn: (seq * chunks + turn, 0, 0)),
        ],
        out_shape=[
            jax.ShapeDtypeStruct((rows, DI), BF),
            jax.ShapeDtypeStruct((rows, DI), BF),
            jax.ShapeDtypeStruct((rows // CHUNK, STATE, DI), BF),
        ],
        scratch_shapes=[
            pltpu.VMEM((STATE, DI), F32),
            pltpu.VMEM((CHUNK + 8, conv_width), F32),
            pltpu.VMEM((CHUNK, DI), F32),
        ],
        compiler_params=pltpu.CompilerParams(
            dimension_semantics=("arbitrary", "arbitrary"), vmem_limit_bytes=48 << 20
        ),
        cost_estimate=pl.CostEstimate(
            flops=30 * rows * DI * 512, bytes_accessed=rows * 24 * 1024, transcendentals=rows * DI
        ),
        name="mix_forward",
    )(proj, raw, *params)


def mix_backward(proj, raw, y, entry, d_mixed, extras, seq_len, seq, earlier, sums):
    rows = proj.shape[0]
    chunks = seq_len // CHUNK
    params = param_rows(extras) + head_maps()
    conv_width = DI + 2 * STATE
    per = CHUNK // 16

    def block(turn):
        return seq * chunks + chunks - 1 - turn

    def at(width):
        return pl.BlockSpec((CHUNK, width), lambda turn: (block(turn), 0))

    def fixed(shape):
        return pl.BlockSpec(shape, lambda turn: (0,) * len(shape))

    small = [(CONV, conv_width), (1, conv_width), (1, DI), (1, DI), (1, HEADS), (1, HEADS)]
    if sums is None:
        sums = [jnp.zeros(shape, F32) for shape in small]
    operands = [proj, proj, raw, y, entry, d_mixed, *params, *sums]
    in_specs = [
        at(proj.shape[1]),
        pl.BlockSpec(
            (16, proj.shape[1]), lambda turn: (jnp.maximum(block(turn) * per - 1, 0), 0)
        ),
        at(HEADS),
        at(DI),
        pl.BlockSpec((1, STATE, DI), lambda turn: (block(turn), 0, 0)),
        at(DI),
    ]
    in_specs += [fixed(item.shape) for item in params + tuple(sums)]
    aliases = {len(operands) - len(small) + k: 1 + k for k in range(len(small))}
    body = bwd_body
    if earlier is not None:
        aliases[len(operands)] = 0
        operands.append(earlier)
        in_specs.append(pl.BlockSpec(memory_space=pl.ANY))
    count = len(operands)

    def run(*refs):
        fixed_count = 6 + len(params)
        bwd_body(*refs[: fixed_count + len(small)], *refs[count:])

    d_proj, *sums = pl.pallas_call(
        run,
        grid=(chunks,),
        in_specs=in_specs,
        out_specs=[at(proj.shape[1])] + [fixed(shape) for shape in small],
        out_shape=[jax.ShapeDtypeStruct(proj.shape, BF)]
        + [jax.ShapeDtypeStruct(shape, F32) for shape in small],
        input_output_aliases=aliases,
        scratch_shapes=[
            pltpu.VMEM((STATE, DI), F32),
            pltpu.VMEM((CHUNK + 8, conv_width), F32),
            pltpu.VMEM((CHUNK + 8, conv_width), F32),
            pltpu.VMEM((CHUNK, conv_width), F32),
            pltpu.VMEM((CHUNK, conv_width), F32),
            pltpu.VMEM((CHUNK, DI), F32),
            pltpu.VMEM((CHUNK, DI), BF),
            pltpu.VMEM((CHUNK, DI), BF),
            pltpu.VMEM((CHUNK, DI), BF),
        ],
        compiler_params=pltpu.CompilerParams(
            dimension_semantics=("arbitrary",), vmem_limit_bytes=48 << 20
        ),
        cost_estimate=pl.CostEstimate(
            flops=70 * seq_len * DI * 512,
            bytes_accessed=seq_len * 40 * 1024,
            transcendentals=seq_len * DI,
        ),
        name="mix_backward",
    )(*operands)
    return d_proj, sums


def rms_scale(values, gain):
    return values * lax.rsqrt(jnp.mean(values * values, axis=-1, keepdims=True) + EPSILON) * gain


def norm_back(values, gain, d_normed):
    scale = lax.rsqrt(jnp.mean(values * values, axis=-1, keepdims=True) + EPSILON)
    scaled = values * scale
    pulled = d_normed * gain
    d_gain = jnp.sum(d_normed * scaled, axis=0)
    d_values = scale * (pulled - scaled * jnp.mean(pulled * scaled, axis=-1, keepdims=True))
    return d_values, d_gain


def tie(*values):
    return lax.optimization_barrier(values)


def gather_rows(shard_rows):
    parts = lax.axis_size("chip") * lax.axis_size("core")
    place = lax.axis_index("chip") * lax.axis_size("core") + lax.axis_index("core")
    count = shard_rows.shape[0] // parts
    mine = lax.dynamic_slice_in_dim(shard_rows, place * count, count, 0)
    return lax.all_gather(mine, ("shard", "chip", "core"), axis=0, tiled=True)


def flip(value, axis, bit=1):
    count = lax.axis_size(axis)
    return lax.ppermute(value, axis, [(place, place ^ bit) for place in range(count)])


def turn(value, axis, shift):
    count = lax.axis_size(axis)
    return lax.ppermute(value, axis, [(place, (place + shift) % count) for place in range(count)])


def add_low(left, right):
    return (left.astype(F32) + right.astype(F32)).astype(BF)


def core_halves(left):
    half = left.shape[1] // lax.axis_size("shard") // 2
    first = lax.axis_index("core") == 0

    def pick(low_first):
        pieces = []
        for start in range(0, left.shape[1], 2 * half):
            low, high = left[:, start : start + half], left[:, start + half : start + 2 * half]
            pieces.append(jnp.where(low_first, low, high))
        return jnp.concatenate(pieces, axis=1)

    return pick(first), pick(~first)


def chip_bits():
    return [1 << k for k in reversed(range(lax.axis_size("chip").bit_length() - 1))]


def spread_blocks(part):
    bits = chip_bits()
    shards = lax.axis_size("shard")
    rows = part.shape[0] // shards >> len(bits)
    return part.reshape((shards,) + (2,) * len(bits) + (rows, part.shape[1]))


def halve(part, bit):
    axis = 1 + chip_bits().index(bit)
    mine = (lax.axis_index("chip") // bit) % 2
    keep = lax.dynamic_index_in_dim(part, mine, axis)
    send = lax.dynamic_index_in_dim(part, 1 - mine, axis)
    return keep, send


class Stages:
    def __init__(self, steps):
        self.steps = steps
        self.sent = next(steps)
        self.result = None

    def advance(self, main):
        if self.sent is None:
            return main
        main, *arrived = tie(main, *self.sent)
        try:
            ready = self.steps.send(arrived)
            main, *ready = tie(main, *ready)
            self.sent = self.steps.send(ready)
        except StopIteration as stop:
            self.sent, self.result = None, stop.value
        return main

    def finish(self):
        while self.sent is not None:
            try:
                ready = self.steps.send(list(self.sent))
                self.sent = self.steps.send(ready)
            except StopIteration as stop:
                self.sent, self.result = None, stop.value
        return self.result


def sum_columns(keeps, sends):
    bits = chip_bits()
    middle = len(bits) // 2
    orders = (bits, bits[middle:] + bits[:middle])
    arrived = yield [flip(send, "core") for send in sends]
    parts = [spread_blocks(add_low(keep, other)) for keep, other in zip(keeps, arrived)]
    for turn_bits in zip(*orders):
        pieces = [halve(part, bit) for part, bit in zip(parts, turn_bits)]
        ready = yield [send for _, send in pieces]
        arrived = yield [flip(send, "chip", bit) for send, bit in zip(ready, turn_bits)]
        parts = [add_low(keep, other) for (keep, _), other in zip(pieces, arrived)]
    shards = lax.axis_size("shard")
    place = lax.axis_index("shard")
    blocks = [part.reshape(shards, -1, part.shape[-1]) for part in parts]

    def block(value, index):
        return lax.dynamic_index_in_dim(value, index % shards, 0, keepdims=False)

    away = [block(value, place + shift) for value in blocks for shift in range(1, shards)]
    ready = yield away
    shifts = [shift for _ in blocks for shift in range(1, shards)]
    arrived = yield [turn(value, "shard", shift) for value, shift in zip(ready, shifts)]
    owned = []
    for k, value in enumerate(blocks):
        total = block(value, place).astype(F32)
        for other in arrived[k * (shards - 1) : (k + 1) * (shards - 1)]:
            total = total + other.astype(F32)
        owned.append(total.astype(BF))
    owned = jnp.concatenate(owned, axis=1)
    return lax.all_gather(owned, ("core", "chip"), axis=0, tiled=True)


def sum_rows(keep, send):
    part = add_low(keep, flip(send, "core"))
    owned = lax.psum_scatter(part, ("shard", "chip"), scatter_dimension=0, tiled=True)
    return lax.all_gather(owned, ("core", "chip"), axis=0, tiled=True)


def sum_everywhere(values):
    sizes = [value.size for value in values]
    flat = jnp.concatenate([value.reshape(-1) for value in values])
    packed = jnp.pad(flat, (0, -flat.size % 1024)).reshape(-1, 128)
    for axis in ("core", "chip", "shard"):
        arrived = [turn(packed, axis, shift) for shift in range(1, lax.axis_size(axis))]
        packed = sum(arrived, packed)
    flat = packed.reshape(-1)
    out, start = [], 0
    for value, size in zip(values, sizes):
        out.append(flat[start : start + size].reshape(value.shape))
        start += size
    return out


def per_device(
    inputs,
    lengths,
    cotangent,
    w_in,
    w_out,
    norm_gain,
    conv_weight,
    conv_bias,
    gate_gain,
    dt_bias,
    a_log,
    skip,
):
    slot_count, seq_len, width = inputs.shape
    row_total = slot_count * seq_len
    places = lax.broadcasted_iota(jnp.int32, (slot_count, seq_len), 1)
    valid_mask = (places < lengths[:, None]).astype(F32).reshape(row_total, 1)
    layer_count = w_in.shape[0]
    raw_start = 2 * DI + 2 * STATE
    full = [(gather_rows(w_in[layer]), gather_rows(w_out[layer])) for layer in range(layer_count)]
    hidden = inputs.reshape(row_total, width)
    saved = []
    for layer in range(layer_count):
        full_in, full_out = full[layer]
        extras = tuple(
            item[layer] for item in (conv_weight, conv_bias, gate_gain, dt_bias, a_log, skip)
        )
        normed = rms_scale(hidden, norm_gain[layer]).astype(BF)
        proj = mm(normed, full_in).astype(BF)
        raw = mm(normed, full_in[:, raw_start:])
        mixed, y, entry = mix_forward(proj, raw, extras, seq_len)
        saved.append((hidden, normed, proj, raw, mixed, y, entry, extras))
        hidden = hidden + valid_mask * mm(mixed, full_out)
    grad_stream = cotangent.reshape(row_total, width)
    grad_stream, mixed_last = tie(grad_stream, saved[-1][4])
    saved[-1] = saved[-1][:4] + (mixed_last,) + saved[-1][5:]
    in_parts = [None] * layer_count
    out_parts = [None] * layer_count
    small_parts = [None] * layer_count
    cut = DI + STATE
    above = None
    for layer in reversed(range(layer_count)):
        below, normed, proj, raw, mixed, y, entry, extras = saved[layer]
        full_in, full_out = full[layer]
        d_branch = (valid_mask * grad_stream).astype(BF)
        keep_left, send_left = core_halves(mixed)
        keep_left, send_out = tie(keep_left, mm_tn(send_left, d_branch).astype(BF))
        d_branch, keep_out = tie(d_branch, mm_tn(keep_left, d_branch).astype(BF))
        out_parts[layer] = sum_rows(keep_out, send_out)
        d_mixed = mm_nt(d_branch, full_out).astype(BF)
        d_proj, smalls = None, None
        for seq in range(slot_count):
            if above is not None:
                d_mixed = above.advance(d_mixed)
            d_proj, smalls = mix_backward(
                proj, raw, y, entry, d_mixed, extras, seq_len, seq, d_proj, smalls
            )
        keep_left, send_left = core_halves(normed)
        if above is not None:
            send_left = above.advance(send_left)
        spans = (d_proj[:, :cut], d_proj[:, cut:])
        sends = [mm_tn(send_left, span).astype(BF) for span in spans]
        keep_left, *sends = tie(keep_left, *sends)
        keeps = [mm_tn(keep_left, span).astype(BF) for span in spans]
        if above is not None:
            in_parts[layer + 1] = above.finish()
        d_proj, *keeps = tie(d_proj, *keeps)
        above = Stages(sum_columns(keeps, sends))
        d_proj = above.advance(d_proj)
        d_hidden, d_gain = norm_back(below, norm_gain[layer], mm_nt(d_proj, full_in))
        grad_stream = grad_stream + d_hidden
        if layer > 0:
            grad_stream = above.advance(grad_stream)
        d_cw, d_cb, d_gg, d_sk, d_dtb, d_al = smalls
        d_skip = jnp.sum(d_sk.reshape(HEADS, HEAD_DIM), axis=1)
        small_parts[layer] = sum_everywhere(
            (d_gain, d_cw, d_cb[0], d_gg[0], d_dtb[0], d_al[0], d_skip)
        )
    in_parts[0] = above.finish()
    stacked = [jnp.stack([small_parts[layer][k] for layer in range(layer_count)]) for k in range(7)]
    return (
        hidden.reshape(slot_count, seq_len, width),
        grad_stream.reshape(slot_count, seq_len, width),
        jnp.stack(in_parts).astype(F32),
        jnp.stack(out_parts).astype(F32),
        *stacked,
    )


def solution(mesh):
    copies, shards = mesh.devices.shape
    mesh = Mesh(mesh.devices.reshape(copies // 2, 2, shards), ("chip", "core", "shard"))
    in_specs = (
        P(("chip", "core", "shard"), None, None),
        P(("chip", "core", "shard")),
        P(("chip", "core", "shard"), None, None),
        P(None, "shard", None),
        P(None, "shard", None),
        P(),
        P(),
        P(),
        P(),
        P(),
        P(),
        P(),
    )
    out_specs = (
        P(("chip", "core", "shard"), None, None),
        P(("chip", "core", "shard"), None, None),
        P(None, "shard", None),
        P(None, "shard", None),
        P(),
        P(),
        P(),
        P(),
        P(),
        P(),
        P(),
    )
    return jax.shard_map(
        per_device, mesh=mesh, in_specs=in_specs, out_specs=out_specs, check_vma=False
    )
```

```python
import jax
import jax.numpy as jnp
from jax import lax
from jax.experimental import pallas as pl
from jax.experimental.pallas import tpu as pltpu
from jax.sharding import Mesh
from jax.sharding import PartitionSpec as P

DI = 2048
HEADS = 32
HEAD_DIM = 64
STATE = 128
CONV = 4
EPSILON = 1e-05
CHUNK = 128
PAIR = 2 * HEAD_DIM
LOG2E = 1.4426950408889634
BF = jnp.bfloat16
F32 = jnp.float32


def dot_f32(left, right, dims, precision=None):
    return lax.dot_general(
        left, right, (dims, ((), ())), preferred_element_type=F32, precision=precision
    )


def mm(left, right):
    return dot_f32(left, right, ((1,), (0,)))


def mm_nt(left, right):
    return dot_f32(left, right, ((1,), (1,)))


def mm_tn(left, right):
    return dot_f32(left, right, ((0,), (0,)))


def split_two(values):
    high = values.astype(BF)
    low = (values - high.astype(F32)).astype(BF)
    return high, low


def block_diag(pair):
    lane = lax.broadcasted_iota(jnp.int32, pair.shape, 1)
    zero = jnp.zeros_like(pair)
    return jnp.concatenate(
        [jnp.where(lane < HEAD_DIM, pair, zero), jnp.where(lane >= HEAD_DIM, pair, zero)], axis=0
    )


def sigmoid(values):
    return 1.0 / (1.0 + jnp.exp(-values))


def softplus(values):
    return jnp.maximum(values, 0.0) + jnp.log1p(jnp.exp(-jnp.abs(values)))


def conv_pre(ext_ref, cw_ref, cb_ref, cols):
    total = cb_ref[:, cols] + cw_ref[0:1, cols] * ext_ref[5 : 5 + CHUNK, cols]
    for tap in range(1, CONV):
        total = total + cw_ref[tap : tap + 1, cols] * ext_ref[5 + tap : 5 + tap + CHUNK, cols]
    return total


def head_terms(raw_ref, dtb_ref, al_ref, spread_ref):
    shifted = raw_ref[...] + dtb_ref[...]
    step = softplus(shifted)
    rate = -jnp.exp(al_ref[...])
    row = lax.broadcasted_iota(jnp.int32, (CHUNK, CHUNK), 0)
    col = lax.broadcasted_iota(jnp.int32, (CHUNK, CHUNK), 1)
    lower = (row >= col).astype(F32)
    cum = dot_f32(lower, step * (rate * LOG2E), ((1,), (0,)), lax.Precision.HIGHEST)
    to_end = jnp.exp2(cum[CHUNK - 1 : CHUNK, :] - cum)

    def spread(values):
        high, low = split_two(values)
        return mm(jnp.concatenate([high, low], axis=1), spread_ref[...])

    return shifted, step, rate, cum, spread(step), spread(to_end), spread(jnp.exp2(cum))


def fwd_body(
    proj_ref, raw_ref, cw_ref, cb_ref, gg_ref, dtb_ref, al_ref, sk_ref, spread_ref,
    mixed_ref, y_ref, entry_ref,
    state, ext, gated,
):
    chunk = pl.program_id(1)

    @pl.when(chunk == 0)
    def _():
        state[...] = jnp.zeros_like(state)
        ext[0:8, :] = jnp.zeros((8, ext.shape[1]), F32)

    @pl.when(chunk != 0)
    def _():
        ext[0:8, :] = ext[CHUNK : CHUNK + 8, :]

    ext[8 : 8 + CHUNK, :] = proj_ref[:, DI : 2 * DI + 2 * STATE].astype(F32)

    def act(start, width):
        pre = conv_pre(ext, cw_ref, cb_ref, slice(start, start + width))
        return pre * sigmoid(pre)

    b_low = act(DI, STATE).astype(BF)
    c_low = act(DI + STATE, STATE).astype(BF)
    _, _, _, cum, step_x, end_x, ecum_x = head_terms(raw_ref, dtb_ref, al_ref, spread_ref)
    cum_t = cum.T
    row = lax.broadcasted_iota(jnp.int32, (CHUNK, CHUNK), 0)
    col = lax.broadcasted_iota(jnp.int32, (CHUNK, CHUNK), 1)
    scores = jnp.where(row >= col, mm_nt(c_low, b_low), 0.0)
    entry_low = state[...].astype(BF)
    entry_ref[0] = entry_low
    b_t = b_low.astype(F32).T.astype(BF)
    squares = jnp.zeros((CHUNK, PAIR), F32)
    for pair in range(HEADS // 2):
        cols = slice(pair * PAIR, (pair + 1) * PAIR)
        x = act(pair * PAIR, PAIR)
        x_step = x * step_x[:, cols]
        mixing = []
        for head in (2 * pair, 2 * pair + 1):
            gap = jnp.minimum(cum[:, head : head + 1] - cum_t[head : head + 1, :], 0.0)
            mixing.append((jnp.exp2(gap) * scores).astype(BF))
        intra = mm(jnp.concatenate(mixing, axis=1), block_diag(x_step.astype(BF)))
        inter = mm(c_low, entry_low[:, cols]) * ecum_x[:, cols]
        y = intra + inter + sk_ref[:, cols] * x
        y_ref[:, cols] = y.astype(BF)
        grown = mm(b_t, (x_step * end_x[:, cols]).astype(BF))
        state[:, cols] = state[:, cols] * ecum_x[CHUNK - 1 : CHUNK, cols] + grown
        z = proj_ref[:, cols].astype(F32)
        g = y * (z * sigmoid(z))
        gated[:, cols] = g
        squares = squares + g * g
    scale = lax.rsqrt(jnp.sum(squares, axis=1, keepdims=True) * (1.0 / DI) + EPSILON)
    for pair in range(HEADS // 2):
        cols = slice(pair * PAIR, (pair + 1) * PAIR)
        mixed_ref[:, cols] = (gated[:, cols] * scale * gg_ref[:, cols]).astype(BF)


def bwd_body(
    proj_ref, before_ref, raw_ref, y_ref, entry_ref, dmix_ref,
    cw_ref, cb_ref, gg_ref, dtb_ref, al_ref, sk_ref, spread_ref, gather_ref,
    cw0_ref, cb0_ref, gg0_ref, sk0_ref, dtb0_ref, al0_ref,
    dproj_ref, dcw_ref, dcb_ref, dgg_ref, dsk_ref, ddtb_ref, dal_ref,
    adj, ext, dpre, act_s, slope_s, dy_s, da_high, da_low, u_s,
):
    turn = pl.program_id(0)
    last = pl.num_programs(0) - 1

    @pl.when(turn == 0)
    def _():
        dcw_ref[...] = cw0_ref[...]
        dcb_ref[...] = cb0_ref[...]
        dgg_ref[...] = gg0_ref[...]
        dsk_ref[...] = sk0_ref[...]
        ddtb_ref[...] = dtb0_ref[...]
        dal_ref[...] = al0_ref[...]

    @pl.when(turn == 0)
    def _():
        adj[...] = jnp.zeros_like(adj)
        dpre[CHUNK : CHUNK + 8, :] = jnp.zeros((8, dpre.shape[1]), F32)

    ext[0:8, :] = jnp.where(
        turn == last, 0.0, before_ref[8:16, DI : 2 * DI + 2 * STATE].astype(F32)
    )
    ext[8 : 8 + CHUNK, :] = proj_ref[:, DI : 2 * DI + 2 * STATE].astype(F32)
    conv_width = DI + 2 * STATE
    for start in range(0, conv_width, PAIR):
        cols = slice(start, start + PAIR)
        pre = conv_pre(ext, cw_ref, cb_ref, cols)
        sig = sigmoid(pre)
        act = pre * sig
        act_s[:, cols] = act
        slope_s[:, cols] = sig + act * (1.0 - sig)

    squares = jnp.zeros((CHUNK, PAIR), F32)
    crossed = jnp.zeros((CHUNK, PAIR), F32)
    for pair in range(HEADS // 2):
        cols = slice(pair * PAIR, (pair + 1) * PAIR)
        z = proj_ref[:, cols].astype(F32)
        g = y_ref[:, cols].astype(F32) * (z * sigmoid(z))
        squares = squares + g * g
        crossed = crossed + dmix_ref[:, cols].astype(F32) * gg_ref[:, cols] * g
    scale = lax.rsqrt(jnp.sum(squares, axis=1, keepdims=True) * (1.0 / DI) + EPSILON)
    pull = scale * scale * scale * (jnp.sum(crossed, axis=1, keepdims=True) * (1.0 / DI))
    for pair in range(HEADS // 2):
        cols = slice(pair * PAIR, (pair + 1) * PAIR)
        z = proj_ref[:, cols].astype(F32)
        y = y_ref[:, cols].astype(F32)
        d_mixed = dmix_ref[:, cols].astype(F32)
        sig = sigmoid(z)
        silu = z * sig
        g = y * silu
        scaled = d_mixed * scale
        d_gated = scaled * gg_ref[:, cols] - g * pull
        dgg_ref[:, cols] += jnp.sum(scaled * g, axis=0, keepdims=True)
        dy_s[:, cols] = d_gated * silu
        dproj_ref[:, cols] = (d_gated * y * (sig + silu * (1.0 - sig))).astype(BF)

    b_low = act_s[:, DI : DI + STATE].astype(BF)
    c_low = act_s[:, DI + STATE :].astype(BF)
    shifted, step, rate, cum, step_x, end_x, ecum_x = head_terms(
        raw_ref, dtb_ref, al_ref, spread_ref
    )
    cum_t = cum.T
    row = lax.broadcasted_iota(jnp.int32, (CHUNK, CHUNK), 0)
    col = lax.broadcasted_iota(jnp.int32, (CHUNK, CHUNK), 1)
    raw_scores = mm_nt(c_low, b_low)
    scores = jnp.where(row >= col, raw_scores, 0.0)
    scores_t = scores.T
    c_t = c_low.astype(F32).T.astype(BF)
    d_scores = jnp.zeros((CHUNK, CHUNK), F32)
    d_c = jnp.zeros((CHUNK, STATE), F32)
    d_b = jnp.zeros((CHUNK, STATE), F32)
    crossing = []
    for pair in range(HEADS // 2):
        cols = slice(pair * PAIR, (pair + 1) * PAIR)
        x = act_s[:, cols]
        dy = dy_s[:, cols]
        step_p = step_x[:, cols]
        x_step = x * step_p
        x_low = x_step.astype(BF)
        dy_low = dy.astype(BF)
        x_bd = block_diag(x_low)
        g_both = mm_nt(dy_low, x_bd)
        mixing = []
        mixing_t = []
        for place, head in enumerate((2 * pair, 2 * pair + 1)):
            down = cum[:, head : head + 1]
            across = cum_t[head : head + 1, :]
            decay = jnp.exp2(jnp.minimum(down - across, 0.0))
            mixing.append((decay * scores).astype(BF))
            d_scores = d_scores + decay * g_both[:, place * CHUNK : (place + 1) * CHUNK]
            decay_t = jnp.exp2(jnp.minimum(across - down, 0.0))
            mixing_t.append((decay_t * scores_t).astype(BF))
        intra = mm(jnp.concatenate(mixing, axis=1), x_bd)
        spread_dy = mm(jnp.concatenate(mixing_t, axis=1), block_diag(dy_low))
        entry = entry_ref[0, :, cols]
        adj_p = adj[:, cols]
        adj_low = adj_p.astype(BF)
        ecum_p = ecum_x[:, cols]
        end_p = end_x[:, cols]
        from_end = mm(b_low, adj_low) * end_p
        y_scan = intra + mm(c_low, entry) * ecum_p
        stuff = spread_dy + from_end
        x_round = x_low.astype(F32)
        u = x_round * stuff
        high, low = split_two(dy_low.astype(F32) * y_scan - u)
        da_high[:, cols] = high
        da_low[:, cols] = low
        u_s[:, cols] = u.astype(BF)
        dy_e = (dy * ecum_p).astype(BF)
        x_e = (x_step * end_p).astype(BF)
        d_c = d_c + mm_nt(dy_e, entry)
        d_b = d_b + mm_nt(x_e, adj_low)
        ecum_last = ecum_x[CHUNK - 1 : CHUNK, cols]
        crossing.append(
            jnp.sum(x_round * from_end, axis=0, keepdims=True)
            + ecum_last * jnp.sum(adj_p * entry.astype(F32), axis=0, keepdims=True)
        )
        adj[:, cols] = adj_p * ecum_last + mm(c_t, dy_e)
        dsk_ref[:, cols] += jnp.sum(dy * x, axis=0, keepdims=True)
        dpre[0:CHUNK, cols] = (step_p * stuff + sk_ref[:, cols] * dy) * slope_s[:, cols]

    through = mm(da_high[...], gather_ref[...]) + mm(da_low[...], gather_ref[...])
    u_head = mm(u_s[...], gather_ref[...])[:, :HEADS]
    cross_row = jnp.broadcast_to(jnp.concatenate(crossing, axis=1), (16, DI))
    cross_high, cross_low = split_two(cross_row)
    cross = (mm(cross_high, gather_ref[...]) + mm(cross_low, gather_ref[...]))[0:1, :HEADS]
    upper = (row <= col).astype(F32)
    d_log = dot_f32(upper, through[:, :HEADS], ((1,), (0,)), lax.Precision.HIGHEST) + cross
    sig = sigmoid(shifted)
    ratio = jnp.where(step > 1e-30, sig / step, 1.0)
    d_raw = u_head * ratio + rate * d_log * sig
    dproj_ref[:, 2 * DI + 2 * STATE :] = d_raw.astype(BF)
    ddtb_ref[...] += jnp.sum(d_raw, axis=0, keepdims=True)
    dal_ref[...] += rate * jnp.sum(step * d_log, axis=0, keepdims=True)

    d_scores = jnp.where(row >= col, d_scores, 0.0)
    d_c = d_c + mm(d_scores.astype(BF), b_low)
    d_b = d_b + mm(d_scores.T.astype(BF), c_low)
    dpre[0:CHUNK, DI : DI + STATE] = d_b * slope_s[:, DI : DI + STATE]
    dpre[0:CHUNK, DI + STATE :] = d_c * slope_s[:, DI + STATE :]
    for start in range(0, conv_width, PAIR):
        cols = slice(start, start + PAIR)
        here = dpre[0:CHUNK, cols]
        d_conv = cw_ref[CONV - 1 : CONV, cols] * here
        dcb_ref[:, cols] += jnp.sum(here, axis=0, keepdims=True)
        for tap in range(CONV):
            dcw_ref[tap : tap + 1, cols] += jnp.sum(
                here * ext[5 + tap : 5 + tap + CHUNK, cols], axis=0, keepdims=True
            )
            if tap < CONV - 1:
                ahead = CONV - 1 - tap
                d_conv = d_conv + cw_ref[tap : tap + 1, cols] * dpre[ahead : ahead + CHUNK, cols]
        dproj_ref[:, DI + start : DI + start + PAIR] = d_conv.astype(BF)
    dpre[CHUNK : CHUNK + 8, :] = dpre[0:8, :]


def head_maps():
    head = jnp.arange(DI) // HEAD_DIM
    spread = (jnp.arange(HEADS)[:, None] == head[None, :]).astype(BF)
    gather = (head[:, None] == jnp.arange(128)[None, :]).astype(BF)
    return jnp.concatenate([spread, spread], axis=0), gather


def whole(array):
    return pl.BlockSpec(array.shape, lambda seq, turn: (0,) * array.ndim)


def param_rows(extras):
    conv_weight, conv_bias, gate_gain, dt_bias, a_log, skip = extras
    return (
        conv_weight,
        conv_bias[None, :],
        gate_gain[None, :],
        dt_bias[None, :],
        a_log[None, :],
        jnp.repeat(skip, HEAD_DIM)[None, :],
    )


def mix_forward(proj, raw, extras, seq_len):
    rows = proj.shape[0]
    seqs, chunks = rows // seq_len, seq_len // CHUNK
    params = param_rows(extras) + (head_maps()[0],)

    def at(width):
        return pl.BlockSpec((CHUNK, width), lambda seq, turn: (seq * chunks + turn, 0))

    conv_width = DI + 2 * STATE
    return pl.pallas_call(
        fwd_body,
        grid=(seqs, chunks),
        in_specs=[at(proj.shape[1]), at(HEADS)] + [whole(item) for item in params],
        out_specs=[
            at(DI),
            at(DI),
            pl.BlockSpec((1, STATE, DI), lambda seq, turn: (seq * chunks + turn, 0, 0)),
        ],
        out_shape=[
            jax.ShapeDtypeStruct((rows, DI), BF),
            jax.ShapeDtypeStruct((rows, DI), BF),
            jax.ShapeDtypeStruct((rows // CHUNK, STATE, DI), BF),
        ],
        scratch_shapes=[
            pltpu.VMEM((STATE, DI), F32),
            pltpu.VMEM((CHUNK + 8, conv_width), F32),
            pltpu.VMEM((CHUNK, DI), F32),
        ],
        compiler_params=pltpu.CompilerParams(
            dimension_semantics=("arbitrary", "arbitrary"), vmem_limit_bytes=48 << 20
        ),
        cost_estimate=pl.CostEstimate(
            flops=30 * rows * DI * 512, bytes_accessed=rows * 24 * 1024, transcendentals=rows * DI
        ),
        name="mix_forward",
    )(proj, raw, *params)


def mix_backward(proj, raw, y, entry, d_mixed, extras, seq_len, seq, earlier, sums):
    rows = proj.shape[0]
    chunks = seq_len // CHUNK
    params = param_rows(extras) + head_maps()
    conv_width = DI + 2 * STATE
    per = CHUNK // 16

    def block(turn):
        return seq * chunks + chunks - 1 - turn

    def at(width):
        return pl.BlockSpec((CHUNK, width), lambda turn: (block(turn), 0))

    def fixed(shape):
        return pl.BlockSpec(shape, lambda turn: (0,) * len(shape))

    small = [(CONV, conv_width), (1, conv_width), (1, DI), (1, DI), (1, HEADS), (1, HEADS)]
    if sums is None:
        sums = [jnp.zeros(shape, F32) for shape in small]
    operands = [proj, proj, raw, y, entry, d_mixed, *params, *sums]
    in_specs = [
        at(proj.shape[1]),
        pl.BlockSpec(
            (16, proj.shape[1]), lambda turn: (jnp.maximum(block(turn) * per - 1, 0), 0)
        ),
        at(HEADS),
        at(DI),
        pl.BlockSpec((1, STATE, DI), lambda turn: (block(turn), 0, 0)),
        at(DI),
    ]
    in_specs += [fixed(item.shape) for item in params + tuple(sums)]
    aliases = {len(operands) - len(small) + k: 1 + k for k in range(len(small))}
    body = bwd_body
    if earlier is not None:
        aliases[len(operands)] = 0
        operands.append(earlier)
        in_specs.append(pl.BlockSpec(memory_space=pl.ANY))
    count = len(operands)

    def run(*refs):
        fixed_count = 6 + len(params)
        bwd_body(*refs[: fixed_count + len(small)], *refs[count:])

    d_proj, *sums = pl.pallas_call(
        run,
        grid=(chunks,),
        in_specs=in_specs,
        out_specs=[at(proj.shape[1])] + [fixed(shape) for shape in small],
        out_shape=[jax.ShapeDtypeStruct(proj.shape, BF)]
        + [jax.ShapeDtypeStruct(shape, F32) for shape in small],
        input_output_aliases=aliases,
        scratch_shapes=[
            pltpu.VMEM((STATE, DI), F32),
            pltpu.VMEM((CHUNK + 8, conv_width), F32),
            pltpu.VMEM((CHUNK + 8, conv_width), F32),
            pltpu.VMEM((CHUNK, conv_width), F32),
            pltpu.VMEM((CHUNK, conv_width), F32),
            pltpu.VMEM((CHUNK, DI), F32),
            pltpu.VMEM((CHUNK, DI), BF),
            pltpu.VMEM((CHUNK, DI), BF),
            pltpu.VMEM((CHUNK, DI), BF),
        ],
        compiler_params=pltpu.CompilerParams(
            dimension_semantics=("arbitrary",), vmem_limit_bytes=48 << 20
        ),
        cost_estimate=pl.CostEstimate(
            flops=seq_len * DI * 512,
            bytes_accessed=seq_len * 10 * 1024,
            transcendentals=seq_len,
        ),
        name="mix_backward",
    )(*operands)
    return d_proj, sums


def assemble_body(place, low_own, low_far, high_own, high_far, out_ref):
    chips = low_own.shape[0]
    rows = low_own.shape[2]
    cut = low_own.shape[3]
    own = pl.program_id(1) == place[0]
    for chip in range(chips):
        far = chip ^ place[1]
        turned = 0
        for bit in range(chips.bit_length() - 1):
            turned = 2 * turned + (far // (1 << bit)) % 2
        span = slice(chip * rows, (chip + 1) * rows)

        @pl.when(own)
        def _():
            out_ref[span, :cut] = low_own[far, 0]
            out_ref[span, cut:] = high_own[turned, 0]

        @pl.when(jnp.logical_not(own))
        def _():
            out_ref[span, :cut] = low_far[far, 0]
            out_ref[span, cut:] = high_far[turned, 0]


def assemble(place, low_own, low_far, high_own, high_far):
    chips, shards, rows, cut = low_own.shape
    rest = high_own.shape[3]

    def blocks(width):
        return pl.BlockSpec(
            (chips, 1, rows, width),
            lambda shard, core, place: (0, (place[2] - shard + shards) % shards, 0, 0),
        )

    return pl.pallas_call(
        assemble_body,
        grid_spec=pltpu.PrefetchScalarGridSpec(
            num_scalar_prefetch=1,
            grid=(shards, 2),
            in_specs=[blocks(cut), blocks(cut), blocks(rest), blocks(rest)],
            out_specs=pl.BlockSpec(
                (chips * rows, cut + rest), lambda shard, core, place: (2 * shard + core, 0)
            ),
        ),
        out_shape=jax.ShapeDtypeStruct((shards * 2 * chips * rows, cut + rest), low_own.dtype),
        compiler_params=pltpu.CompilerParams(
            dimension_semantics=("arbitrary", "arbitrary"), vmem_limit_bytes=48 << 20
        ),
        name="assemble",
    )(place, low_own, low_far, high_own, high_far)


def widen_body(low_ref, *refs):
    refs[-1][0] = low_ref[...].astype(F32)


def widen_turned_body(low_ref, *refs):
    for start in range(0, low_ref.shape[1], 128):
        stop = min(start + 128, low_ref.shape[1])
        refs[-1][0, start:stop, :] = low_ref[:, start:stop].astype(F32).T


def widen(low, layer, layers, earlier, turned):
    rows, width = low.shape
    tile = min(rows, 128)
    operands, specs, aliases = [low], [pl.BlockSpec((tile, width), lambda k: (k, 0))], {}
    if earlier is not None:
        operands.append(earlier)
        specs.append(pl.BlockSpec(memory_space=pl.ANY))
        aliases = {1: 0}
    if turned:
        shape = (layers, width, rows)
        out_spec = pl.BlockSpec((1, width, tile), lambda k: (layer, 0, k))
    else:
        shape = (layers, rows, width)
        out_spec = pl.BlockSpec((1, tile, width), lambda k: (layer, k, 0))
    return pl.pallas_call(
        widen_turned_body if turned else widen_body,
        grid=(rows // tile,),
        in_specs=specs,
        out_specs=out_spec,
        out_shape=jax.ShapeDtypeStruct(shape, F32),
        input_output_aliases=aliases,
        compiler_params=pltpu.CompilerParams(
            dimension_semantics=("arbitrary",), vmem_limit_bytes=48 << 20
        ),
        name="widen",
    )(*operands)


def rms_scale(values, gain):
    return values * lax.rsqrt(jnp.mean(values * values, axis=-1, keepdims=True) + EPSILON) * gain


def norm_back(values, gain, d_normed):
    scale = lax.rsqrt(jnp.mean(values * values, axis=-1, keepdims=True) + EPSILON)
    scaled = values * scale
    pulled = d_normed * gain
    d_gain = jnp.sum(d_normed * scaled, axis=0)
    d_values = scale * (pulled - scaled * jnp.mean(pulled * scaled, axis=-1, keepdims=True))
    return d_values, d_gain


def tie(*values):
    return lax.optimization_barrier(values)


def gather_rows(shard_rows):
    parts = lax.axis_size("chip") * lax.axis_size("core")
    place = lax.axis_index("chip") * lax.axis_size("core") + lax.axis_index("core")
    count = shard_rows.shape[0] // parts
    mine = lax.dynamic_slice_in_dim(shard_rows, place * count, count, 0)
    return lax.all_gather(mine, ("shard", "chip", "core"), axis=0, tiled=True)


def flip(value, axis, bit=1):
    count = lax.axis_size(axis)
    return lax.ppermute(value, axis, [(place, place ^ bit) for place in range(count)])


def turn(value, axis, shift):
    count = lax.axis_size(axis)
    return lax.ppermute(value, axis, [(place, (place + shift) % count) for place in range(count)])


def add_low(left, right):
    return (left.astype(F32) + right.astype(F32)).astype(BF)


def core_halves(left):
    half = left.shape[1] // lax.axis_size("shard") // 2
    first = lax.axis_index("core") == 0

    def pick(low_first):
        pieces = []
        for start in range(0, left.shape[1], 2 * half):
            low, high = left[:, start : start + half], left[:, start + half : start + 2 * half]
            pieces.append(jnp.where(low_first, low, high))
        return jnp.concatenate(pieces, axis=1)

    return pick(first), pick(~first)


def chip_bits():
    return [1 << k for k in reversed(range(lax.axis_size("chip").bit_length() - 1))]


def spread_blocks(part):
    bits = chip_bits()
    shards = lax.axis_size("shard")
    rows = part.shape[0] // shards >> len(bits)
    return part.reshape((shards,) + (2,) * len(bits) + (rows, part.shape[1]))


def halve(part, bit):
    axis = 1 + chip_bits().index(bit)
    mine = (lax.axis_index("chip") // bit) % 2
    keep = lax.dynamic_index_in_dim(part, mine, axis)
    send = lax.dynamic_index_in_dim(part, 1 - mine, axis)
    return keep, send


class Stages:
    def __init__(self, steps):
        self.steps = steps
        self.sent = next(steps)
        self.result = None

    def advance(self, main):
        if self.sent is None:
            return main
        main, *arrived = tie(main, *self.sent)
        try:
            ready = self.steps.send(arrived)
            main, *ready = tie(main, *ready)
            self.sent = self.steps.send(ready)
        except StopIteration as stop:
            self.sent, self.result = None, stop.value
        return main

    def finish(self):
        while self.sent is not None:
            try:
                ready = self.steps.send(list(self.sent))
                self.sent = self.steps.send(ready)
            except StopIteration as stop:
                self.sent, self.result = None, stop.value
        return self.result


def sum_columns(keeps, sends):
    bits = chip_bits()
    middle = len(bits) // 2
    orders = (bits, bits[middle:] + bits[:middle])
    arrived = yield [flip(send, "core") for send in sends]
    parts = [spread_blocks(add_low(keep, other)) for keep, other in zip(keeps, arrived)]
    for turn_bits in zip(*orders):
        pieces = [halve(part, bit) for part, bit in zip(parts, turn_bits)]
        ready = yield [send for _, send in pieces]
        arrived = yield [flip(send, "chip", bit) for send, bit in zip(ready, turn_bits)]
        parts = [add_low(keep, other) for (keep, _), other in zip(pieces, arrived)]
    shards = lax.axis_size("shard")
    place = lax.axis_index("shard")
    blocks = [part.reshape(shards, -1, part.shape[-1]) for part in parts]

    def block(value, index):
        return lax.dynamic_index_in_dim(value, index % shards, 0, keepdims=False)

    away = [block(value, place + shift) for value in blocks for shift in range(1, shards)]
    ready = yield away
    shifts = [shift for _ in blocks for shift in range(1, shards)]
    arrived = yield [turn(value, "shard", shift) for value, shift in zip(ready, shifts)]
    owned = []
    for k, value in enumerate(blocks):
        total = block(value, place).astype(F32)
        for other in arrived[k * (shards - 1) : (k + 1) * (shards - 1)]:
            total = total + other.astype(F32)
        owned.append(total.astype(BF))
    owned = jnp.concatenate(owned, axis=1)
    return lax.all_gather(owned, ("core", "chip"), axis=0, tiled=True)


def gather_in_stages(shard_rows, cut):
    chips = lax.axis_size("chip")
    core, chip, shard = (lax.axis_index(axis) for axis in ("core", "chip", "shard"))
    count = shard_rows.shape[0] // (2 * chips)
    mine = lax.dynamic_slice_in_dim(shard_rows, (core * chips + chip) * count, count, 0)
    others = [turn(mine, "shard", shift) for shift in range(1, lax.axis_size("shard"))]
    line = jnp.stack([mine] + others)[None]
    bits = [1 << k for k in range(chips.bit_length() - 1)]
    spans = [line[..., :cut], line[..., cut:]]
    orders = (bits, bits[::-1])
    near = []
    for step in range(len(bits)):
        spans = [(span, flip(span, "chip", order[step])) for span, order in zip(spans, orders)]
        spans = [jnp.concatenate(pair, axis=0) for pair in spans]
    low, high = spans
    far = [flip(span, "core") for span in (low, high)]
    place = jnp.stack([core, chip, shard]).astype(jnp.int32)
    return assemble(place, low, far[0], high, far[1])


def sum_rows(part):
    axes = ("shard", "chip")
    ready = yield [lax.psum_scatter(part, axes, scatter_dimension=0, tiled=True)]
    ready = yield ready
    arrived = yield [lax.all_gather(ready[0], ("core", "chip"), axis=0, tiled=True)]
    return arrived[0]


def sum_everywhere(values):
    sizes = [value.size for value in values]
    flat = jnp.concatenate([value.reshape(-1) for value in values])
    packed = jnp.pad(flat, (0, -flat.size % 1024)).reshape(-1, 128)
    for axis in ("core", "chip", "shard"):
        arrived = [turn(packed, axis, shift) for shift in range(1, lax.axis_size(axis))]
        packed = sum(arrived, packed)
    flat = packed.reshape(-1)
    out, start = [], 0
    for value, size in zip(values, sizes):
        out.append(flat[start : start + size].reshape(value.shape))
        start += size
    return out


def per_device(
    inputs,
    lengths,
    cotangent,
    w_in,
    w_out,
    norm_gain,
    conv_weight,
    conv_bias,
    gate_gain,
    dt_bias,
    a_log,
    skip,
):
    slot_count, seq_len, width = inputs.shape
    row_total = slot_count * seq_len
    places = lax.broadcasted_iota(jnp.int32, (slot_count, seq_len), 1)
    valid_mask = (places < lengths[:, None]).astype(F32).reshape(row_total, 1)
    layer_count = w_in.shape[0]
    raw_start = 2 * DI + 2 * STATE
    all_in = [gather_rows(w_in[layer]) for layer in range(layer_count)]
    all_out = [gather_in_stages(w_out[0], width // 2)]
    all_in[0], all_out[0] = tie(all_in[0], all_out[0])
    hidden = inputs.reshape(row_total, width)
    saved = []
    for layer in range(layer_count):
        full_in, full_out = all_in[layer], all_out[layer]
        extras = tuple(
            item[layer] for item in (conv_weight, conv_bias, gate_gain, dt_bias, a_log, skip)
        )
        normed = rms_scale(hidden, norm_gain[layer]).astype(BF)
        proj = mm(normed, full_in).astype(BF)
        raw = mm(normed, full_in[:, raw_start:])
        if layer + 1 < layer_count:
            proj, rows_next = tie(proj, w_out[layer + 1])
            all_out.append(gather_rows(rows_next))
        mixed, y, entry = mix_forward(proj, raw, extras, seq_len)
        saved.append((hidden, normed, proj, raw, mixed, y, entry, extras))
        hidden = hidden + valid_mask * mm(mixed, full_out)
    grad_stream = cotangent.reshape(row_total, width)
    grad_in, grad_out = None, None
    small_parts = [None] * layer_count
    cut = DI + STATE
    above = None
    for layer in reversed(range(layer_count)):
        below, normed, proj, raw, mixed, y, entry, extras = saved[layer]
        full_in, full_out = all_in[layer], all_out[layer]
        d_branch = (valid_mask * grad_stream).astype(BF)
        keep_left, send_left = core_halves(mixed)
        keep_left, send_out = tie(keep_left, mm_tn(send_left, d_branch).astype(BF))
        keep_out = mm_tn(keep_left, d_branch).astype(BF)
        part_out = add_low(keep_out, flip(send_out, "core"))
        d_branch, part_out, full_out = tie(d_branch, part_out, full_out)
        beside = Stages(sum_rows(part_out))
        d_mixed = mm_nt(d_branch, full_out).astype(BF)
        d_proj, smalls = None, None
        for seq in range(slot_count):
            if above is not None:
                d_mixed = above.advance(d_mixed)
            d_proj, smalls = mix_backward(
                proj, raw, y, entry, d_mixed, extras, seq_len, seq, d_proj, smalls
            )
        keep_left, send_left = core_halves(normed)
        if above is not None:
            send_left = above.advance(send_left)
        send_left = beside.advance(send_left)
        spans = (d_proj[:, :cut], d_proj[:, cut:])
        sends = [mm_tn(send_left, span).astype(BF) for span in spans]
        keep_left, *sends = tie(keep_left, *sends)
        keeps = [mm_tn(keep_left, span).astype(BF) for span in spans]
        if above is not None:
            grad_in = widen(above.finish(), layer + 1, layer_count, grad_in, True)
        d_proj, *keeps = tie(d_proj, *keeps)
        above = Stages(sum_columns(keeps, sends))
        d_proj = above.advance(d_proj)
        d_normed = mm_nt(d_proj, full_in)
        if layer == 0:
            d_normed = above.advance(d_normed)
        d_hidden, d_gain = norm_back(below, norm_gain[layer], d_normed)
        grad_stream = grad_stream + d_hidden
        grad_stream = above.advance(grad_stream)
        if layer > 0:
            grad_stream = beside.advance(grad_stream)
        grad_out = widen(beside.finish(), layer, layer_count, grad_out, False)
        d_cw, d_cb, d_gg, d_sk, d_dtb, d_al = smalls
        d_skip = jnp.sum(d_sk.reshape(HEADS, HEAD_DIM), axis=1)
        small_parts[layer] = sum_everywhere(
            (d_gain, d_cw, d_cb[0], d_gg[0], d_dtb[0], d_al[0], d_skip)
        )
    grad_in = widen(above.finish(), 0, layer_count, grad_in, True)
    stacked = [jnp.stack([small_parts[layer][k] for layer in range(layer_count)]) for k in range(7)]
    return (
        hidden.reshape(slot_count, seq_len, width),
        grad_stream.reshape(slot_count, seq_len, width),
        jnp.swapaxes(grad_in, 1, 2),
        grad_out,
        *stacked,
    )


def solution(mesh):
    copies, shards = mesh.devices.shape
    mesh = Mesh(mesh.devices.reshape(copies // 2, 2, shards), ("chip", "core", "shard"))
    in_specs = (
        P(("chip", "core", "shard"), None, None),
        P(("chip", "core", "shard")),
        P(("chip", "core", "shard"), None, None),
        P(None, "shard", None),
        P(None, "shard", None),
        P(),
        P(),
        P(),
        P(),
        P(),
        P(),
        P(),
    )
    out_specs = (
        P(("chip", "core", "shard"), None, None),
        P(("chip", "core", "shard"), None, None),
        P(None, "shard", None),
        P(None, "shard", None),
        P(),
        P(),
        P(),
        P(),
        P(),
        P(),
        P(),
    )
    return jax.shard_map(
        per_device, mesh=mesh, in_specs=in_specs, out_specs=out_specs, check_vma=False
    )
```
